256 devices in a mesh: section: 8 (over x, y_hi), tile: 32 (over z, y_lo, core).
Axes of the slice: x: 4, y: 4 (y_hi: 2, y_lo: 2; y = y_hi * 2 + y_lo), z: 8, core: 2. Of those that a mesh axis runs over, the one named last changes fastest.
Arguments:
- carried_act: bfloat16 [8, 192, 16, 16, 256], P('section', 'tile'), may hold values from -6 to 6
- stored_out: bfloat16 [8, 192, 16, 16, 256], P('section', 'tile'), may hold values from -6 to 6
- cotangent: bfloat16 [8, 192, 16, 16, 256], P('section', 'tile'), may hold values from -6 to 6
- weights: bfloat16 [8, 2, 27, 128, 128], P('section'), may hold values from -0.109375 to 0.109375
- momentum: float32 [8, 2, 27, 128, 128], P('section'), may hold values from -6 to 6
Outputs:
- forward_out: bfloat16 [8, 192, 16, 16, 256], P('section', 'tile')
- input_grad: bfloat16 [8, 192, 16, 16, 256], P('section', 'tile')
- new_momentum: float32 [8, 2, 27, 128, 128], P('section')
The draws below stay inside these ranges and needn't reach their ends.
All inputs are finite; a program needn't handle non-finite values.
Results may differ from the reference program's by a relative error of at most 0.006.
Values may be sent and summed in bfloat16 or wider, within the bound.
No kernel may reach another device: no remote copies, remote signals or barrier semaphores. Data moves between devices by JAX's collectives and lax.ppermute only.
A program may use at most 128 MiB of HBM per device.

```python
import jax
import jax.numpy as jnp
from jax import lax

HALF = 128
HY = 16
WX = 16
SECTIONS = 8
NZ = 192


def block_scale(own_key, dims, split, low, high):
    loudness, own = 1.0, jax.random.fold_in(own_key, 6)
    for axis_at, parts in split:
        draws = jnp.exp(jax.random.uniform(jax.random.fold_in(own, axis_at), (parts,), jnp.float32, low / len(split), high / len(split)))
        loudness = loudness * jnp.repeat(draws, dims[axis_at] // parts).reshape([-1 if axis == axis_at else 1 for axis in range(len(dims))])
    return loudness


def bell_draw(key, shape, spread, reach, split=(), dtype=jnp.bfloat16):
    loudness = block_scale(key, shape, split, -0.22, 0.18) if split else 1.0
    array = jax.random.normal(key, shape, jnp.float32) * spread * loudness
    return jnp.minimum(jnp.maximum(array, -reach), reach).astype(dtype)


def setup_inputs(seed: int = 0) -> dict:
    key_list = jax.random.split(jax.random.key(seed), 6)
    carried_act = bell_draw(key_list[0], (SECTIONS, NZ, HY, WX, 2 * HALF), 1.0, 6.0, ((0, 8), (1, 32)))
    stored_out = bell_draw(key_list[1], (SECTIONS, NZ, HY, WX, 2 * HALF), 1.0, 6.0, ((0, 8), (1, 32)))
    cotangent = bell_draw(key_list[2], (SECTIONS, NZ, HY, WX, 2 * HALF), 1.0, 6.0, ((0, 8), (1, 32)))
    weights = bell_draw(key_list[3], (SECTIONS, 2, 27, HALF, HALF), (27 * HALF) ** -0.5, 0.109375, ((0, 8),))
    momentum = bell_draw(key_list[4], (SECTIONS, 2, 27, HALF, HALF), 1.0, 6.0, ((0, 8),), jnp.float32)
    return dict(carried_act=carried_act, stored_out=stored_out, cotangent=cotangent, weights=weights, momentum=momentum)


momentum_decay = 0.9
grad_weight = 0.25

def flatten(field):
    return field.reshape(-1, field.shape[-1])

def columns(padded, depth, rows, cols):
    pieces = []
    for i in range(3):
        for j in range(3):
            for k in range(3):
                pieces.append(padded[i:i + depth, j:j + rows, k:k + cols, :])
    return flatten(jnp.concatenate(pieces, axis=-1))

def unfold(field):
    depth, rows, cols, chans = field.shape
    padded = jnp.pad(field, ((1, 1), (1, 1), (1, 1), (0, 0)))
    return columns(padded, depth, rows, cols)

def convolve(unfolded, weight):
    return jnp.dot(unfolded, weight.reshape(-1, weight.shape[-1]), preferred_element_type=jnp.float32)

def flipped(weight):
    return jnp.transpose(jnp.flip(weight, 0), (0, 2, 1))

def section_step(fwd_in, stored, coming, weight):
    half = weight.shape[-1]
    shape = fwd_in.shape[:3] + (half,)
    w_f = weight[0]
    w_g = weight[1]
    a_one = fwd_in[..., :half]
    a_two = fwd_in[..., half:]
    f_val = jnp.tanh(convolve(unfold(a_two), w_f)).reshape(shape)
    b_one = (a_one.astype(jnp.float32) + f_val).astype(jnp.bfloat16)
    g_val = jnp.tanh(convolve(unfold(b_one), w_g)).reshape(shape)
    b_two = (a_two.astype(jnp.float32) + g_val).astype(jnp.bfloat16)
    out_fwd = jnp.concatenate([b_one, b_two], axis=-1)
    z_one = stored[..., :half]
    z_two = stored[..., half:]
    c_one = coming[..., :half]
    c_two = coming[..., half:]
    cols_z = unfold(z_one)
    g_rec = jnp.tanh(convolve(cols_z, w_g)).reshape(shape)
    r_two = (z_two.astype(jnp.float32) - g_rec).astype(jnp.bfloat16)
    cols_r = unfold(r_two)
    f_rec = jnp.tanh(convolve(cols_r, w_f)).reshape(shape)
    pre_g = (c_two.astype(jnp.float32) * (1.0 - g_rec * g_rec)).astype(jnp.bfloat16)
    d_one = (c_one.astype(jnp.float32) + convolve(unfold(pre_g), flipped(w_g)).reshape(shape)).astype(jnp.bfloat16)
    pre_f = (d_one.astype(jnp.float32) * (1.0 - f_rec * f_rec)).astype(jnp.bfloat16)
    d_two = (c_two.astype(jnp.float32) + convolve(unfold(pre_f), flipped(w_f)).reshape(shape)).astype(jnp.bfloat16)
    out_grad = jnp.concatenate([d_one, d_two], axis=-1)
    grad_f = jnp.dot(cols_r.T, flatten(pre_f), preferred_element_type=jnp.float32)
    grad_g = jnp.dot(cols_z.T, flatten(pre_g), preferred_element_type=jnp.float32)
    grads = jnp.stack([grad_f, grad_g]).reshape(weight.shape)
    return (out_fwd, out_grad, grads)

def reference(carried_act, stored_out, cotangent, weights, momentum):
    fwd_in = jnp.roll(carried_act, 1, axis=0)
    coming = jnp.roll(cotangent, -1, axis=0)

    def one(items):
        return section_step(items[0], items[1], items[2], items[3])
    out_fwd, out_grad, grads = lax.map(one, (fwd_in, stored_out, coming, weights))
    total = NZ * HY * WX
    grads = grads * (grad_weight / jnp.sqrt(jnp.float32(total)))
    new_momentum = momentum_decay * momentum + grads
    return (out_fwd, out_grad, new_momentum)
```

```python
import functools

import jax
import jax.numpy as jnp
from jax import lax
from jax.experimental import pallas as pl
from jax.experimental.pallas import tpu as pltpu
from jax.sharding import PartitionSpec as P

momentum_decay = 0.9
grad_weight = 0.25
bf16 = jnp.bfloat16
f32 = jnp.float32
CELLS = 256
ROW = 16
TILES = 32
STEP = 288
VMEM_LIMIT = 60 << 20


def sides(layer):
    cell = lax.broadcasted_iota(jnp.int32, layer.shape, 0) % ROW
    before = jnp.where(cell == 0, 0.0, pltpu.roll(layer, 1, 0))
    after = jnp.where(cell == ROW - 1, 0.0, pltpu.roll(layer, CELLS - 1, 0))
    return before, after


def expand(wide, at, layer):
    before, after = sides(layer)
    start = at * STEP
    if not isinstance(at, int):
        start = pl.multiple_of(start, STEP)
    blank = jnp.zeros((ROW, 384), bf16)
    wide[pl.ds(start, ROW), :] = blank
    wide[pl.ds(start + STEP - ROW, ROW), :] = blank
    body = pl.ds(start + ROW, CELLS)
    wide[body, 0:128] = before.astype(bf16)
    wide[body, 128:256] = layer.astype(bf16)
    wide[body, 256:384] = after.astype(bf16)


def convolve(wide, at, taps):
    pieces = []
    for i in range(3):
        for j in range(3):
            start = (at + i) * STEP + j * ROW
            if not isinstance(at, int):
                start = pl.multiple_of(start, ROW)
            pieces.append(wide[pl.ds(start, CELLS), :])
    return jnp.dot(jnp.concatenate(pieces, axis=1), taps[...], preferred_element_type=f32)


def turn(flat, at, layer):
    before, after = sides(layer)
    place = pl.ds(at * CELLS, CELLS)
    flat[0:128, place] = before.T.astype(bf16)
    flat[128:256, place] = layer.T.astype(bf16)
    flat[256:384, place] = after.T.astype(bf16)


def layer_of(ref, at, low):
    return ref[at, :, :, low : low + 128].reshape(CELLS, 128)


def stored_kernel(place, z, z_low, z_high, w_g, g_out, r_out, z_wide, taps_g):
    first = place[0] == 0
    last = place[0] == TILES - 1
    taps_g[...] = w_g[0, 0].reshape(27 * 128, 128)
    for at in range(10):
        if at < 2:
            one = jnp.where(first, 0.0, layer_of(z_low, at, 0).astype(f32))
        elif at < 8:
            one = layer_of(z, at - 2, 0).astype(f32)
        else:
            one = jnp.where(last, 0.0, layer_of(z_high, at - 8, 0).astype(f32))
        expand(z_wide, at, one)
    for at in range(8):
        g_rec = jnp.tanh(convolve(z_wide, at, taps_g))
        if at == 0:
            two = jnp.where(first, 0.0, layer_of(z_low, 1, 128).astype(f32) - g_rec)
        elif at < 7:
            two = layer_of(z, at - 1, 128).astype(f32) - g_rec
            g_out[at - 1] = 1.0 - g_rec * g_rec
        else:
            two = jnp.where(last, 0.0, layer_of(z_high, 0, 128).astype(f32) - g_rec)
        r_out[at] = two.astype(bf16)


def inner_kernel(place, z, z_low, z_high, r, w_f, w_g, f_out, z_flat, r_flat, g_turned, f_turned, r_wide, taps_f):
    first = place[0] == 0
    last = place[0] == TILES - 1
    taps_f[...] = w_f[0, 0].reshape(27 * 128, 128)
    for at in range(8):
        two = r[at].astype(f32)
        expand(r_wide, at, two)
        turn(r_flat, at, two)
        if at == 0:
            one = jnp.where(first, 0.0, layer_of(z_low, 1, 0).astype(f32))
        elif at < 7:
            one = layer_of(z, at - 1, 0).astype(f32)
        else:
            one = jnp.where(last, 0.0, layer_of(z_high, 0, 0).astype(f32))
        turn(z_flat, at, one)
    for at in range(6):
        f_rec = jnp.tanh(convolve(r_wide, at, taps_f))
        f_out[at] = 1.0 - f_rec * f_rec
    for tap in range(27):
        rows = slice(tap * 128, tap * 128 + 128)
        g_turned[rows, :] = w_g[0, 0, 26 - tap].astype(f32).T.astype(bf16)
        f_turned[rows, :] = w_f[0, 0, 26 - tap].astype(f32).T.astype(bf16)


def gradient(place, flat, d_of, mine, other, d_pad, d_all, parts):
    blank = jnp.zeros((ROW, 128), bf16)
    for at in range(6):
        d_pad[at * STEP : at * STEP + ROW, :] = blank
        d_pad[(at + 1) * STEP - ROW : (at + 1) * STEP, :] = blank
        d_pad[at * STEP + ROW : at * STEP + ROW + CELLS, :] = d_of(at)
    for at in range(6):
        for j in range(3):
            start = at * STEP + (2 - j) * ROW
            d_all[at * CELLS : (at + 1) * CELLS, j * 128 : j * 128 + 128] = d_pad[start : start + CELLS, :]
    core = place[0] % 2
    deep = place[0] // 4
    for i in range(3):
        part = jnp.dot(flat[:, i * CELLS : (i + 6) * CELLS], d_all[...], preferred_element_type=f32)
        for j in range(3):
            for k in range(3):
                block = part[k * 128 : k * 128 + 128, j * 128 : j * 128 + 128].astype(bf16)
                parts[9 * i + 3 * j + k] = block
    for m in range(4):
        for out, ahead in ((mine, core * (m - 3) + (1 - core) * (4 - m)), (other, (1 - core) * (m - 3) + core * (4 - m))):
            rows = pl.ds(pl.multiple_of(((deep + ahead + 8) % 8) * 16, 16), 16)
            out[m] = parts[:, rows, :]


def grad_g_kernel(place, z_flat, pg, mine, other, d_pad, d_all, parts):
    gradient(place, z_flat, lambda at: layer_of(pg, at, 0), mine, other, d_pad, d_all, parts)


def first_kernel(place, pg, pg_low, pg_high, c_one, f_scale, taps, r_flat, d_out, pf_out, mine, other, wide, d_pad, d_all, parts):
    first = place[0] == 0
    last = place[0] == TILES - 1
    expand(wide, 0, jnp.where(first, 0.0, layer_of(pg_low, 0, 0).astype(f32)))
    expand(wide, 7, jnp.where(last, 0.0, layer_of(pg_high, 0, 0).astype(f32)))
    for at in range(6):
        expand(wide, at + 1, layer_of(pg, at, 0).astype(f32))
    for at in range(6):
        d_one = (layer_of(c_one, at, 0).astype(f32) + convolve(wide, at, taps)).astype(bf16)
        d_out[at] = d_one.reshape(16, 16, 128)
        pf_out[at] = (d_one.astype(f32) * f_scale[at]).astype(bf16).reshape(16, 16, 128)
    gradient(place, r_flat, lambda at: layer_of(pf_out, at, 0), mine, other, d_pad, d_all, parts)


def second_kernel(place, pf, pf_low, pf_high, c_two, d_one, taps, out, wide):
    first = place[0] == 0
    last = place[0] == TILES - 1
    expand(wide, 0, jnp.where(first, 0.0, layer_of(pf_low, 0, 0).astype(f32)))
    expand(wide, 7, jnp.where(last, 0.0, layer_of(pf_high, 0, 0).astype(f32)))
    for at in range(6):
        expand(wide, at + 1, layer_of(pf, at, 0).astype(f32))
    for at in range(6):
        d_two = (layer_of(c_two, at, 0).astype(f32) + convolve(wide, at, taps)).astype(bf16)
        out[0, at, :, :, 0:128] = d_one[at]
        out[0, at, :, :, 128:256] = d_two.reshape(16, 16, 128)


def forward_kernel(place, a, a_low, a_high, w_f, w_g, out, a_wide, b_wide, taps_f, taps_g):
    first = place[0] == 0
    last = place[0] == TILES - 1
    taps_f[...] = w_f[0, 0].reshape(27 * 128, 128)
    taps_g[...] = w_g[0, 0].reshape(27 * 128, 128)
    for at in range(10):
        if at < 2:
            two = jnp.where(first, 0.0, layer_of(a_low, at, 128).astype(f32))
        elif at < 8:
            two = layer_of(a, at - 2, 128).astype(f32)
        else:
            two = jnp.where(last, 0.0, layer_of(a_high, at - 8, 128).astype(f32))
        expand(a_wide, at, two)
    for at in range(8):
        f_val = jnp.tanh(convolve(a_wide, at, taps_f))
        if at == 0:
            one = jnp.where(first, 0.0, layer_of(a_low, 1, 0).astype(f32) + f_val)
        elif at < 7:
            one = layer_of(a, at - 1, 0).astype(f32) + f_val
        else:
            one = jnp.where(last, 0.0, layer_of(a_high, 0, 0).astype(f32) + f_val)
        one = one.astype(bf16)
        if 1 <= at < 7:
            out[0, at - 1, :, :, 0:128] = one.reshape(16, 16, 128)
        expand(b_wide, at, one.astype(f32))
    for at in range(6):
        g_val = jnp.tanh(convolve(b_wide, at, taps_g))
        two = (layer_of(a, at, 128).astype(f32) + g_val).astype(bf16)
        out[0, at, :, :, 128:256] = two.reshape(16, 16, 128)


def momentum_kernel(scale, place, momentum, *refs):
    chunks, out = refs[:8], refs[-1]
    core = place[0] % 2
    deep = place[0] // 4
    sign = jnp.where(core == 0, 7, 1)
    eighths = [deep, deep + sign, deep + 2 * sign, deep + 3 * sign, deep + 4]
    eighths += [deep + 8 - sign, deep + 2 * (8 - sign), deep + 3 * (8 - sign)]
    for chunk, eighth in zip(chunks, eighths):
        rows = pl.ds(pl.multiple_of((eighth % 8) * 16, 16), 16)
        out[0, 0, :, rows, :] = momentum_decay * momentum[0, 0, :, rows, :] + chunk[...].astype(f32) * scale


VMEM = pl.BlockSpec(memory_space=pltpu.VMEM)
SMEM = pl.BlockSpec(memory_space=pltpu.SMEM)


def taps_of(which):
    return pl.BlockSpec((1, 1, 27, 128, 128), lambda _: (0, which, 0, 0, 0))


def cost(layers):
    flops = layers * CELLS * 27 * 128 * 128 * 2
    return pl.CostEstimate(flops=flops, bytes_accessed=6_000_000, transcendentals=0)


def call(kernel, specs, outs, scratch, layers):
    return pl.pallas_call(
        kernel,
        grid=(1,),
        in_specs=specs,
        out_specs=[VMEM] * len(outs),
        out_shape=[jax.ShapeDtypeStruct(shape, kind) for shape, kind in outs],
        scratch_shapes=[pltpu.VMEM(shape, kind) for shape, kind in scratch],
        compiler_params=pltpu.CompilerParams(vmem_limit_bytes=VMEM_LIMIT),
        cost_estimate=cost(layers),
    )


def along(block, distance):
    count = lax.axis_size("section")
    return lax.ppermute(block, "section", [((i - distance) % count, i) for i in range(count)])


def halo(low_block, high_block):
    count = lax.axis_size("tile")
    low = lax.ppermute(low_block, "tile", [(i, (i + 1) % count) for i in range(count)])
    high = lax.ppermute(high_block, "tile", [((i + 1) % count, i) for i in range(count)])
    return low, high


def tiles(target):
    route = []
    for i in range(lax.axis_size("tile")):
        deep, near, core = target(i // 4, i // 2 % 2, i % 2)
        route.append((i, (deep % 8) * 4 + near * 2 + core))
    return route


def sent(block, target):
    return lax.ppermute(block, "tile", tiles(target))


def swapped(block):
    return sent(block, lambda z, y, c: (z, y, 1 - c))


def onward(block):
    return sent(block, lambda z, y, c: (z + 1 - 2 * c, y, c))


def reduced(mine, other):
    from_core = swapped(other)

    def own(m):
        return mine[m].astype(f32) + from_core[m].astype(f32)

    held = own(0).astype(bf16)
    for m in (1, 2, 3):
        held = (own(m) + onward(held).astype(f32)).astype(bf16)
    straight = sent(held, lambda z, y, c: (z + 1 - c, y, c))
    across = sent(held, lambda z, y, c: (z + 1 - c, 1 - y, c))
    held = (straight.astype(f32) + across.astype(f32)).astype(bf16)
    held = (held.astype(f32) + swapped(held).astype(f32)).astype(bf16)
    chunks = [held]
    for _ in range(4):
        chunks.append(onward(chunks[-1]))
    return chunks + [swapped(chunk) for chunk in chunks[1:4]]


def shards(carried_act, stored_out, cotangent, weights, momentum):
    half = 128
    field = (6, 16, 16, half)
    count = lax.axis_size("tile")
    total = stored_out.shape[1] * count * stored_out.shape[2] * stored_out.shape[3]
    place = lax.axis_index("tile").reshape(1)
    z = stored_out[0]
    z_low, z_high = halo(z[4:], z[:2])
    c_two = along(cotangent[0, ..., half:], -1)
    late, z_low, z_high = lax.optimization_barrier((cotangent[0, ..., :half], z_low, z_high))
    c_one = along(late, -1)
    wide10, wide8 = ((10 * STEP, 384), bf16), ((8 * STEP, 384), bf16)
    taps = ((27 * half, half), bf16)
    flat = ((384, 8 * CELLS), bf16)
    padded, all_d = ((6 * STEP, half), bf16), ((6 * CELLS, 384), bf16)
    eighths, parts = ((4, 27, 16, half), bf16), ((27, half, half), bf16)
    scales = ((6, CELLS, half), f32)
    g_scale, r = call(
        stored_kernel,
        [SMEM, VMEM, VMEM, VMEM, taps_of(1)],
        [scales, ((8, CELLS, half), bf16)],
        [wide10, taps],
        8,
    )(place, z, z_low, z_high, weights)
    pg = (c_two.astype(f32) * g_scale.reshape(field)).astype(bf16)
    pg_low, pg_high = halo(pg[5:], pg[:1])
    f_scale, z_flat, r_flat, g_turned, f_turned = call(
        inner_kernel,
        [SMEM, VMEM, VMEM, VMEM, VMEM, taps_of(0), taps_of(1)],
        [scales, flat, flat, taps, taps],
        [wide8, taps],
        6,
    )(place, z, z_low, z_high, r, weights, weights)
    mine_g, other_g = call(grad_g_kernel, [SMEM, VMEM, VMEM], [eighths] * 2, [padded, all_d, parts], 6)(place, z_flat, pg)
    act, pg_low, pg_high = lax.optimization_barrier((carried_act[0], pg_low, pg_high))
    a = along(act, 1)
    d_one, pf, mine_f, other_f = call(
        first_kernel,
        [SMEM] + [VMEM] * 7,
        [(field, bf16), (field, bf16), eighths, eighths],
        [wide8, padded, all_d, parts],
        12,
    )(place, pg, pg_low, pg_high, c_one, f_scale, g_turned, r_flat)
    grad_f = reduced(mine_f, other_f)
    grad_g = reduced(mine_g, other_g)
    pf_low, pf_high = halo(pf[5:], pf[:1])
    a_low, a_high = halo(a[4:], a[:2])
    whole = ((1, 6, 16, 16, 2 * half), bf16)
    (out_grad,) = call(second_kernel, [SMEM] + [VMEM] * 6, [whole], [wide8], 6)(
        place, pf, pf_low, pf_high, c_two, d_one, f_turned
    )
    (out_fwd,) = call(
        forward_kernel,
        [SMEM, VMEM, VMEM, VMEM, taps_of(0), taps_of(1)],
        [whole],
        [wide10, wide8, taps, taps],
        14,
    )(place, a, a_low, a_high, weights, weights)
    scale = grad_weight / float(total) ** 0.5
    new = None
    for which, chunks in ((1, grad_g), (0, grad_f)):
        spec = pl.BlockSpec((1, 1, 27, half, half), functools.partial(lambda at, _: (0, at, 0, 0, 0), which))
        kept = [] if new is None else [new]
        new = pl.pallas_call(
            functools.partial(momentum_kernel, scale),
            grid=(1,),
            in_specs=[SMEM, spec] + [VMEM] * 8 + [pl.BlockSpec(memory_space=pl.ANY)] * len(kept),
            out_specs=spec,
            out_shape=jax.ShapeDtypeStruct(momentum.shape, f32),
            input_output_aliases={10: 0} if kept else {},
            compiler_params=pltpu.CompilerParams(vmem_limit_bytes=VMEM_LIMIT),
            cost_estimate=pl.CostEstimate(flops=1_000_000, bytes_accessed=4_400_000, transcendentals=0),
        )(place, momentum, *chunks, *kept)
    return (out_fwd, out_grad, new)


def solution(mesh):
    placed = (
        P("section", "tile", None, None, None),
        P("section", "tile", None, None, None),
        P("section", "tile", None, None, None),
        P("section", None, None, None, None),
        P("section", None, None, None, None),
    )
    return jax.shard_map(
        shards,
        mesh=mesh,
        in_specs=placed,
        out_specs=(
            P("section", "tile", None, None, None),
            P("section", "tile", None, None, None),
            P("section", None, None, None, None),
        ),
        check_vma=False,
    )
```

```python
import functools

import jax
import jax.numpy as jnp
from jax import lax
from jax.experimental import pallas as pl
from jax.experimental.pallas import tpu as pltpu
from jax.sharding import PartitionSpec as P

momentum_decay = 0.9
grad_weight = 0.25
bf16 = jnp.bfloat16
f32 = jnp.float32
CELLS = 256
ROW = 16
TILES = 32
STEP = 288
VMEM_LIMIT = 28 << 20


def sides(layer):
    cell = lax.broadcasted_iota(jnp.int32, layer.shape, 0) % ROW
    before = jnp.where(cell == 0, 0.0, pltpu.roll(layer, 1, 0))
    after = jnp.where(cell == ROW - 1, 0.0, pltpu.roll(layer, CELLS - 1, 0))
    return before, after


def expand(wide, at, layer):
    before, after = sides(layer)
    start = pl.multiple_of(at * STEP, ROW)
    blank = jnp.zeros((ROW, 384), bf16)
    wide[pl.ds(start, ROW), :] = blank
    wide[pl.ds(start + STEP - ROW, ROW), :] = blank
    body = pl.ds(start + ROW, CELLS)
    wide[body, 0:128] = before.astype(bf16)
    wide[body, 128:256] = layer.astype(bf16)
    wide[body, 256:384] = after.astype(bf16)


def convolve(wide, at, taps):
    pieces = []
    for i in range(3):
        for j in range(3):
            start = [pl.multiple_of((at + i + h) * STEP + j * ROW, ROW) for h in range(2)]
            pieces.append(jnp.concatenate([wide[pl.ds(rows, CELLS), :] for rows in start], axis=0))
    return jnp.dot(jnp.concatenate(pieces, axis=1), taps[...], preferred_element_type=f32)


def pairs(count, body):
    def step(at, carry):
        body(at * 2)
        return carry

    lax.fori_loop(0, count // 2, step, 0)


def each(count, body):
    def step(at, carry):
        body(at)
        return carry

    lax.fori_loop(0, count, step, 0)


def half_of(value, h):
    return value[h * CELLS : h * CELLS + CELLS]


def turn(flat, at, layer):
    before, after = sides(layer)
    place = pl.ds(pl.multiple_of(at * CELLS, CELLS), CELLS)
    flat[0:128, place] = before.T.astype(bf16)
    flat[128:256, place] = layer.T.astype(bf16)
    flat[256:384, place] = after.T.astype(bf16)


def gather(to, low, mid, high, place, channel, reach):
    first = place[0] == 0
    last = place[0] == TILES - 1
    for at in range(reach):
        to[at] = jnp.where(first, 0.0, layer_of(low, low.shape[0] - reach + at, channel).astype(f32)).astype(bf16)
        to[6 + reach + at] = jnp.where(last, 0.0, layer_of(high, at, channel).astype(f32)).astype(bf16)

    def copy(at):
        to[at + reach] = layer_of(mid, at, channel)

    each(6, copy)


def outside(place, at):
    return jnp.logical_or(
        jnp.logical_and(at == 0, place[0] == 0), jnp.logical_and(at == 7, place[0] == TILES - 1)
    )


def layer_of(ref, at, low):
    return ref[at, :, :, low : low + 128].reshape(CELLS, 128)


def stored_kernel(place, z, z_low, z_high, w_g, g_out, r_out, z_wide, taps_g, ones, twos):
    taps_g[...] = w_g[0, 0].reshape(27 * 128, 128)
    gather(ones, z_low, z, z_high, place, 0, 2)
    gather(twos, z_low, z, z_high, place, 128, 1)
    each(10, lambda at: expand(z_wide, at, ones[at].astype(f32)))

    def step(at):
        g_rec = jnp.tanh(convolve(z_wide, at, taps_g))
        for h in range(2):
            part = half_of(g_rec, h)
            g_out[at + h] = 1.0 - part * part
            two = twos[at + h].astype(f32) - part
            r_out[at + h] = jnp.where(outside(place, at + h), 0.0, two).astype(bf16)

    pairs(8, step)


def turned_kernel(w, w_turned):
    def turned(tap):
        rows = pl.ds(pl.multiple_of(tap * 128, 128), 128)
        w_turned[rows, :] = w[0, 0, 26 - tap].astype(f32).T.astype(bf16)

    each(27, turned)


def inner_kernel(place, z, z_low, z_high, r, w_f, f_out, z_flat, r_flat, r_wide, taps_f, ones):
    taps_f[...] = w_f[0, 0].reshape(27 * 128, 128)
    gather(ones, z_low, z, z_high, place, 0, 1)

    def prepare(at):
        two = r[at].astype(f32)
        expand(r_wide, at, two)
        turn(r_flat, at, two)
        turn(z_flat, at, ones[at].astype(f32))

    each(8, prepare)

    def step(at):
        f_rec = jnp.tanh(convolve(r_wide, at, taps_f))
        for h in range(2):
            part = half_of(f_rec, h)
            f_out[at + h] = 1.0 - part * part

    pairs(6, step)


def gradient(place, flat, d_of, mine, other, d_pad, d_all, parts):
    blank = jnp.zeros((ROW, 128), bf16)

    def pad(at):
        start = pl.multiple_of(at * STEP, ROW)
        d_pad[pl.ds(start, ROW), :] = blank
        d_pad[pl.ds(start + STEP - ROW, ROW), :] = blank
        d_pad[pl.ds(start + ROW, CELLS), :] = d_of(at)
        rows = pl.ds(pl.multiple_of(at * CELLS, CELLS), CELLS)
        for j in range(3):
            d_all[rows, j * 128 : j * 128 + 128] = d_pad[pl.ds(start + (2 - j) * ROW, CELLS), :]

    each(6, pad)
    for i in range(3):
        part = jnp.dot(flat[:, i * CELLS : (i + 6) * CELLS], d_all[...], preferred_element_type=f32)
        for j in range(3):
            for k in range(3):
                block = part[k * 128 : k * 128 + 128, j * 128 : j * 128 + 128].astype(bf16)
                parts[9 * i + 3 * j + k] = block
    core = place[0] % 2
    deep = place[0] // 4

    def hand(m):
        near, far = 4 - m, m + 5
        for out, ahead in ((mine, jnp.where(core == 0, near, far)), (other, jnp.where(core == 0, far, near))):
            rows = pl.ds(pl.multiple_of(((deep + ahead) % 8) * 16, 16), 16)
            out[m, 0] = parts[:, rows, :]

    each(4, hand)


def grad_g_kernel(place, z_flat, pg, mine, other, d_pad, d_all, parts):
    gradient(place, z_flat, lambda at: layer_of(pg, at, 0), mine, other, d_pad, d_all, parts)


def widen(wide, low, mid, high, place, layers):
    gather(layers, low, mid, high, place, 0, 1)
    each(8, lambda at: expand(wide, at, layers[at].astype(f32)))


def first_kernel(place, pg, pg_low, pg_high, c_one, f_scale, taps, r_flat, mine_in, other_in, d_out, pf_out, mine, other, wide, d_pad, d_all, parts, layers):
    widen(wide, pg_low, pg, pg_high, place, layers)

    def step(at):
        value = convolve(wide, at, taps)
        for h in range(2):
            d_one = (layer_of(c_one, at + h, 0).astype(f32) + half_of(value, h)).astype(bf16)
            d_out[0, at + h] = d_one.reshape(16, 16, 128)
            pf_out[at + h] = (d_one.astype(f32) * f_scale[at + h]).astype(bf16).reshape(16, 16, 128)

    pairs(6, step)
    gradient(place, r_flat, lambda at: layer_of(pf_out, at, 0), mine, other, d_pad, d_all, parts)


def second_kernel(place, pf, pf_low, pf_high, c_two, taps, d_one, out, wide, layers):
    widen(wide, pf_low, pf, pf_high, place, layers)

    def step(at):
        value = convolve(wide, at, taps)
        for h in range(2):
            d_two = (layer_of(c_two, at + h, 0).astype(f32) + half_of(value, h)).astype(bf16)
            out[0, at + h] = d_two.reshape(16, 16, 128)

    pairs(6, step)


def b_one_kernel(place, a, a_low, a_high, w_f, b_out, a_wide, taps_f, ones, twos):
    taps_f[...] = w_f[0, 0].reshape(27 * 128, 128)
    gather(ones, a_low, a, a_high, place, 0, 1)
    gather(twos, a_low, a, a_high, place, 128, 2)
    each(10, lambda at: expand(a_wide, at, twos[at].astype(f32)))

    def step(at):
        f_val = jnp.tanh(convolve(a_wide, at, taps_f))
        for h in range(2):
            one = ones[at + h].astype(f32) + half_of(f_val, h)
            b_out[at + h] = jnp.where(outside(place, at + h), 0.0, one).astype(bf16)

    pairs(8, step)


def b_two_kernel(a, b, w_g, out, b_wide, taps_g):
    taps_g[...] = w_g[0, 0].reshape(27 * 128, 128)
    each(8, lambda at: expand(b_wide, at, b[at].astype(f32)))

    def step(at):
        g_val = jnp.tanh(convolve(b_wide, at, taps_g))
        for h in range(2):
            two = (layer_of(a, at + h, 128).astype(f32) + half_of(g_val, h)).astype(bf16)
            out[0, at + h, :, :, 0:128] = b[at + h + 1].reshape(16, 16, 128)
            out[0, at + h, :, :, 128:256] = two.reshape(16, 16, 128)

    pairs(6, step)


def momentum_kernel(scale, count, places, momentum, *refs):
    out = refs[-1]
    for at in range(count):

        @pl.when(pl.program_id(0) == at)
        def _():
            out[0] = momentum_decay * momentum[0] + refs[at][...].astype(f32) * scale


VMEM = pl.BlockSpec(memory_space=pltpu.VMEM)
SMEM = pl.BlockSpec(memory_space=pltpu.SMEM)


def taps_of(which):
    return pl.BlockSpec((1, 1, 27, 128, 128), lambda _: (0, which, 0, 0, 0))


def cost(layers):
    flops = layers * CELLS * 27 * 128 * 128 * 2
    return pl.CostEstimate(flops=flops, bytes_accessed=6_000_000, transcendentals=0)


def call(kernel, specs, outs, scratch, layers, out_specs=None, aliases=None):
    return pl.pallas_call(
        kernel,
        grid=(1,),
        in_specs=specs,
        out_specs=out_specs or [VMEM] * len(outs),
        out_shape=[jax.ShapeDtypeStruct(shape, kind) for shape, kind in outs],
        scratch_shapes=[pltpu.VMEM(shape, kind) for shape, kind in scratch],
        input_output_aliases=aliases or {},
        compiler_params=pltpu.CompilerParams(vmem_limit_bytes=VMEM_LIMIT),
        cost_estimate=cost(layers),
    )


def along(block, distance):
    count = lax.axis_size("section")
    return lax.ppermute(block, "section", [((i - distance) % count, i) for i in range(count)])


def halo(low_block, high_block):
    count = lax.axis_size("tile")
    low = lax.ppermute(low_block, "tile", [(i, (i + 1) % count) for i in range(count)])
    high = lax.ppermute(high_block, "tile", [((i + 1) % count, i) for i in range(count)])
    return low, high


def tiles(target):
    route = []
    for i in range(lax.axis_size("tile")):
        deep, near, core = target(i // 4, i // 2 % 2, i % 2)
        route.append((i, (deep % 8) * 4 + near * 2 + core))
    return route


def sent(block, target):
    return lax.ppermute(block, "tile", tiles(target))


def swapped(block):
    return sent(block, lambda z, y, c: (z, y, 1 - c))


def onward(block):
    return sent(block, lambda z, y, c: (z + 1 - 2 * c, y, c))


def tied(*values):
    return lax.optimization_barrier(values)


def updated(momentum, kept, chunks, places, scale):
    count = len(chunks)
    spec = pl.BlockSpec((1, 2, 27, 16, 128), lambda at, places: (0, 0, 0, places[at], 0))
    anywhere = pl.BlockSpec(memory_space=pl.ANY)
    return pl.pallas_call(
        functools.partial(momentum_kernel, scale, count),
        grid_spec=pltpu.PrefetchScalarGridSpec(
            num_scalar_prefetch=1,
            grid=(count,),
            in_specs=[spec] + [pl.BlockSpec((2, 27, 16, 128), lambda at, places: (0, 0, 0, 0))] * count + [anywhere] * len(kept),
            out_specs=spec,
        ),
        out_shape=jax.ShapeDtypeStruct(momentum.shape, f32),
        input_output_aliases={count + 2: 0} if kept else {},
        compiler_params=pltpu.CompilerParams(vmem_limit_bytes=VMEM_LIMIT),
        cost_estimate=pl.CostEstimate(flops=1_000_000, bytes_accessed=1_100_000 * count, transcendentals=0),
    )(places, momentum, *chunks, *kept)


def shards(carried_act, stored_out, cotangent, weights, momentum):
    half = 128
    field = (6, 16, 16, half)
    count = lax.axis_size("tile")
    total = stored_out.shape[1] * count * stored_out.shape[2] * stored_out.shape[3]
    scale = grad_weight / float(total) ** 0.5
    place = lax.axis_index("tile").reshape(1)
    core, deep = place[0] % 2, place[0] // 4
    wide10, wide8 = ((10 * STEP, 384), bf16), ((8 * STEP, 384), bf16)
    taps = ((27 * half, half), bf16)
    flat = ((384, 8 * CELLS), bf16)
    padded, all_d = ((6 * STEP, half), bf16), ((6 * CELLS, 384), bf16)
    eighths, parts = ((4, 2, 27, 16, half), bf16), ((27, half, half), bf16)
    ten, eight = ((10, CELLS, half), bf16), ((8, CELLS, half), bf16)
    whole = ((1, 6, 16, 16, 2 * half), bf16)
    anywhere = pl.BlockSpec(memory_space=pl.ANY)

    z = stored_out[0]
    c_two = along(cotangent[0, ..., half:], -1)
    z_low, z_high = halo(z[4:], z[:2])
    (g_turned,) = call(turned_kernel, [taps_of(1)], [taps], [], 1)(weights)
    z_low, z_high, g_turned = tied(z_low, z_high, g_turned)
    g_scale, r = call(
        stored_kernel,
        [SMEM, VMEM, VMEM, VMEM, taps_of(1)],
        [((8, CELLS, half), f32), eight],
        [wide10, taps, ten, eight],
        8,
    )(place, z, z_low, z_high, weights)
    late, r = tied(cotangent[0, ..., :half], r)
    c_one = along(late, -1)
    pg = (c_two.astype(f32) * g_scale[1:7].reshape(field)).astype(bf16)
    pg, r = tied(pg, r)
    pg_low, pg_high = halo(pg[5:], pg[:1])
    f_scale, z_flat, r_flat = call(
        inner_kernel,
        [SMEM, VMEM, VMEM, VMEM, VMEM, taps_of(0)],
        [((6, CELLS, half), f32), flat, flat],
        [wide8, taps, eight],
        6,
    )(place, z, z_low, z_high, r, weights)

    def side(which):
        return pl.BlockSpec((1, 6, 16, 16, half), lambda _: (0, 0, 0, 0, which))

    def part(which):
        return pl.BlockSpec((4, 1, 27, 16, half), lambda _: (0, which, 0, 0, 0))

    mine, other = call(
        grad_g_kernel, [SMEM, VMEM, VMEM], [eighths] * 2, [padded, all_d, parts], 6, [part(1), part(1)]
    )(place, z_flat, pg)
    act, pg_low, pg_high = tied(carried_act[0], pg_low, pg_high)
    a = along(act, 1)
    d_one, pf, mine, other = call(
        first_kernel,
        [SMEM] + [VMEM] * 7 + [anywhere] * 2,
        [whole, (field, bf16), eighths, eighths],
        [wide8, padded, all_d, parts, eight],
        12,
        [side(0), VMEM, part(0), part(0)],
        {8: 2, 9: 3},
    )(place, pg, pg_low, pg_high, c_one, f_scale, g_turned, r_flat, mine, other)

    from_core = swapped(other)
    from_core, weights_later = tied(from_core, weights)
    pf_low, pf_high = halo(pf[5:], pf[:1])

    def own(m):
        return mine[m].astype(f32) + from_core[m].astype(f32)

    sign = jnp.where(core == 0, 7, 1)
    steps = jnp.stack([0 * sign, sign, -sign, 2 * sign, -2 * sign, 3 * sign, -3 * sign, 4 * sign])
    places = (deep + steps + 32) % 8
    got = onward(own(0).astype(bf16))
    (f_turned,) = call(turned_kernel, [taps_of(0)], [taps], [], 1)(weights_later)
    got, places, f_turned, pf_low, pf_high = tied(got, places, f_turned, pf_low, pf_high)
    got = onward((own(1) + got.astype(f32)).astype(bf16))
    got = onward((own(2) + got.astype(f32)).astype(bf16))
    got, a = tied(got, a)
    a_low, a_high = halo(a[4:], a[:2])
    held = (own(3) + got.astype(f32)).astype(bf16)
    straight = sent(held, lambda z, y, c: (z + 1 - c, y, c))
    across = sent(held, lambda z, y, c: (z + 1 - c, 1 - y, c))
    held = (straight.astype(f32) + across.astype(f32)).astype(bf16)
    held = (held.astype(f32) + swapped(held).astype(f32)).astype(bf16)
    first = onward(held)
    (out_grad,) = call(
        second_kernel, [SMEM] + [VMEM] * 5 + [anywhere], [whole], [wide8, eight], 6, [side(1)], {6: 0}
    )(place, pf, pf_low, pf_high, c_two, f_turned, d_one)
    first, a_low, a_high, out_grad = tied(first, a_low, a_high, out_grad)
    second = onward(first)
    first_other = swapped(first)
    (b_one,) = call(
        b_one_kernel, [SMEM, VMEM, VMEM, VMEM, taps_of(0)], [eight], [wide10, taps, eight, ten], 8
    )(place, a, a_low, a_high, weights)
    second, first_other, b_one = tied(second, first_other, b_one)
    third = onward(second)
    second_other = swapped(second)
    (out_fwd,) = call(b_two_kernel, [VMEM, VMEM, taps_of(1)], [whole], [wide8, taps], 6)(a, b_one, weights)
    third, second_other, out_fwd = tied(third, second_other, out_fwd)
    fourth = onward(third)
    third_other = swapped(third)
    new = updated(momentum, [], [held, first, first_other, second, second_other], places[:5], scale)
    fourth, third_other, new = tied(fourth, third_other, new)
    new = updated(momentum, [new], [third, third_other, fourth], places[5:], scale)
    return (out_fwd, out_grad, new)


def solution(mesh):
    placed = (
        P("section", "tile", None, None, None),
        P("section", "tile", None, None, None),
        P("section", "tile", None, None, None),
        P("section", None, None, None, None),
        P("section", None, None, None, None),
    )
    return jax.shard_map(
        shards,
        mesh=mesh,
        in_specs=placed,
        out_specs=(
            P("section", "tile", None, None, None),
            P("section", "tile", None, None, None),
            P("section", None, None, None, None),
        ),
        check_vma=False,
    )
```

```python
import functools

import jax
import jax.numpy as jnp
from jax import lax
from jax.experimental import pallas as pl
from jax.experimental.pallas import tpu as pltpu
from jax.sharding import PartitionSpec as P

momentum_decay = 0.9
grad_weight = 0.25
bf16 = jnp.bfloat16
f32 = jnp.float32
CELLS = 256
ROW = 16
TILES = 32
STEP = 288
VMEM_LIMIT = 28 << 20


def sides(layer):
    cell = lax.broadcasted_iota(jnp.int32, layer.shape, 0) % ROW
    before = jnp.where(cell == 0, 0.0, pltpu.roll(layer, 1, 0))
    after = jnp.where(cell == ROW - 1, 0.0, pltpu.roll(layer, CELLS - 1, 0))
    return before, after


def expand(wide, at, layer):
    before, after = sides(layer)
    start = pl.multiple_of(at * STEP, ROW)
    blank = jnp.zeros((ROW, 384), bf16)
    wide[pl.ds(start, ROW), :] = blank
    wide[pl.ds(start + STEP - ROW, ROW), :] = blank
    body = pl.ds(start + ROW, CELLS)
    wide[body, 0:128] = before.astype(bf16)
    wide[body, 128:256] = layer.astype(bf16)
    wide[body, 256:384] = after.astype(bf16)


def convolve(wide, at, taps):
    pieces = []
    for i in range(3):
        for j in range(3):
            start = [pl.multiple_of((at + i + h) * STEP + j * ROW, ROW) for h in range(2)]
            pieces.append(jnp.concatenate([wide[pl.ds(rows, CELLS), :] for rows in start], axis=0))
    return jnp.dot(jnp.concatenate(pieces, axis=1), taps[...], preferred_element_type=f32)


def pairs(count, body):
    def step(at, carry):
        body(at * 2)
        return carry

    lax.fori_loop(0, count // 2, step, 0)


def each(count, body):
    def step(at, carry):
        body(at)
        return carry

    lax.fori_loop(0, count, step, 0)


def half_of(value, h):
    return value[h * CELLS : h * CELLS + CELLS]


def turn(flat, at, layer):
    before, after = sides(layer)
    place = pl.ds(pl.multiple_of(at * CELLS, CELLS), CELLS)
    flat[0:128, place] = before.T.astype(bf16)
    flat[128:256, place] = layer.T.astype(bf16)
    flat[256:384, place] = after.T.astype(bf16)


def gather(to, low, mid, high, place, channel, reach):
    first = place[0] == 0
    last = place[0] == TILES - 1
    for at in range(reach):
        to[at] = jnp.where(first, 0.0, layer_of(low, low.shape[0] - reach + at, channel).astype(f32)).astype(bf16)
        to[6 + reach + at] = jnp.where(last, 0.0, layer_of(high, at, channel).astype(f32)).astype(bf16)

    def copy(at):
        to[at + reach] = layer_of(mid, at, channel)

    each(6, copy)


def outside(place, at):
    return jnp.logical_or(
        jnp.logical_and(at == 0, place[0] == 0), jnp.logical_and(at == 7, place[0] == TILES - 1)
    )


def layer_of(ref, at, low):
    return ref[at, :, :, low : low + 128].reshape(CELLS, 128)


def stored_kernel(place, z, z_low, z_high, w_g, g_out, r_out, z_wide, taps_g, ones, twos):
    taps_g[...] = w_g[0, 0].reshape(27 * 128, 128)
    gather(ones, z_low, z, z_high, place, 0, 2)
    gather(twos, z_low, z, z_high, place, 128, 1)
    each(10, lambda at: expand(z_wide, at, ones[at].astype(f32)))

    def step(at):
        g_rec = jnp.tanh(convolve(z_wide, at, taps_g))
        for h in range(2):
            part = half_of(g_rec, h)
            g_out[at + h] = 1.0 - part * part
            two = twos[at + h].astype(f32) - part
            r_out[at + h] = jnp.where(outside(place, at + h), 0.0, two).astype(bf16)

    pairs(8, step)


def cut_kernel(z, c, top, bottom, c_one, c_two):
    for at in range(2):
        top[at] = z[at + 4]
        bottom[at] = z[at]
    for at in range(6):
        c_one[at] = c[at, :, :, 0:128]
        c_two[at] = c[at, :, :, 128:256]


def turned_kernel(w, w_turned):
    def turned(tap):
        rows = pl.ds(pl.multiple_of(tap * 128, 128), 128)
        w_turned[rows, :] = w[0, 0, 26 - tap].astype(f32).T.astype(bf16)

    each(27, turned)


def inner_kernel(place, z, z_low, z_high, r, w_f, f_out, z_flat, r_flat, r_wide, taps_f, ones):
    taps_f[...] = w_f[0, 0].reshape(27 * 128, 128)
    gather(ones, z_low, z, z_high, place, 0, 1)

    def prepare(at):
        two = r[at].astype(f32)
        expand(r_wide, at, two)
        turn(r_flat, at, two)
        turn(z_flat, at, ones[at].astype(f32))

    each(8, prepare)

    def step(at):
        f_rec = jnp.tanh(convolve(r_wide, at, taps_f))
        for h in range(2):
            part = half_of(f_rec, h)
            f_out[at + h] = 1.0 - part * part

    pairs(6, step)


def gradient(place, flat, d_of, mine, other, d_pad, d_all, parts):
    blank = jnp.zeros((ROW, 128), bf16)

    def pad(at):
        start = pl.multiple_of(at * STEP, ROW)
        d_pad[pl.ds(start, ROW), :] = blank
        d_pad[pl.ds(start + STEP - ROW, ROW), :] = blank
        d_pad[pl.ds(start + ROW, CELLS), :] = d_of(at)
        rows = pl.ds(pl.multiple_of(at * CELLS, CELLS), CELLS)
        for j in range(3):
            d_all[rows, j * 128 : j * 128 + 128] = d_pad[pl.ds(start + (2 - j) * ROW, CELLS), :]

    each(6, pad)
    for i in range(3):
        part = jnp.dot(flat[:, i * CELLS : (i + 6) * CELLS], d_all[...], preferred_element_type=f32)
        for j in range(3):
            for k in range(3):
                block = part[k * 128 : k * 128 + 128, j * 128 : j * 128 + 128].astype(bf16)
                parts[9 * i + 3 * j + k] = block
    core = place[0] % 2
    deep = place[0] // 4

    def hand(m):
        near, far = 4 - m, m + 5
        for out, ahead in ((mine, jnp.where(core == 0, near, far)), (other, jnp.where(core == 0, far, near))):
            rows = pl.ds(pl.multiple_of(((deep + ahead) % 8) * 16, 16), 16)
            out[m, 0] = parts[:, rows, :]

    each(4, hand)


def grad_g_kernel(place, z_flat, pg, mine, other, d_pad, d_all, parts):
    gradient(place, z_flat, lambda at: layer_of(pg, at, 0), mine, other, d_pad, d_all, parts)


def widen(wide, low, mid, high, place, layers):
    gather(layers, low, mid, high, place, 0, 1)
    each(8, lambda at: expand(wide, at, layers[at].astype(f32)))


def first_kernel(place, pg, pg_low, pg_high, c_one, f_scale, taps, r_flat, mine_in, other_in, d_out, pf_out, mine, other, wide, d_pad, d_all, parts, layers):
    widen(wide, pg_low, pg, pg_high, place, layers)

    def step(at):
        value = convolve(wide, at, taps)
        for h in range(2):
            d_one = (layer_of(c_one, at + h, 0).astype(f32) + half_of(value, h)).astype(bf16)
            d_out[0, at + h] = d_one.reshape(16, 16, 128)
            pf_out[at + h] = (d_one.astype(f32) * f_scale[at + h]).astype(bf16).reshape(16, 16, 128)

    pairs(6, step)
    gradient(place, r_flat, lambda at: layer_of(pf_out, at, 0), mine, other, d_pad, d_all, parts)


def second_kernel(place, pf, pf_low, pf_high, c_two, taps, d_one, out, wide, layers):
    widen(wide, pf_low, pf, pf_high, place, layers)

    def step(at):
        value = convolve(wide, at, taps)
        for h in range(2):
            d_two = (layer_of(c_two, at + h, 0).astype(f32) + half_of(value, h)).astype(bf16)
            out[0, at + h] = d_two.reshape(16, 16, 128)

    pairs(6, step)


def b_one_kernel(place, a, a_low, a_high, w_f, b_out, a_wide, taps_f, ones, twos):
    taps_f[...] = w_f[0, 0].reshape(27 * 128, 128)
    gather(ones, a_low, a, a_high, place, 0, 1)
    gather(twos, a_low, a, a_high, place, 128, 2)
    each(10, lambda at: expand(a_wide, at, twos[at].astype(f32)))

    def step(at):
        f_val = jnp.tanh(convolve(a_wide, at, taps_f))
        for h in range(2):
            one = ones[at + h].astype(f32) + half_of(f_val, h)
            b_out[at + h] = jnp.where(outside(place, at + h), 0.0, one).astype(bf16)

    pairs(8, step)


def b_two_kernel(a, b, w_g, out, b_wide, taps_g):
    taps_g[...] = w_g[0, 0].reshape(27 * 128, 128)
    each(8, lambda at: expand(b_wide, at, b[at].astype(f32)))

    def step(at):
        g_val = jnp.tanh(convolve(b_wide, at, taps_g))
        for h in range(2):
            two = (layer_of(a, at + h, 128).astype(f32) + half_of(g_val, h)).astype(bf16)
            out[0, at + h, :, :, 0:128] = b[at + h + 1].reshape(16, 16, 128)
            out[0, at + h, :, :, 128:256] = two.reshape(16, 16, 128)

    pairs(6, step)


def momentum_kernel(scale, count, places, momentum, *refs):
    out = refs[-1]
    for at in range(count):

        @pl.when(pl.program_id(0) == at)
        def _():
            out[0] = momentum_decay * momentum[0] + refs[at][...].astype(f32) * scale


VMEM = pl.BlockSpec(memory_space=pltpu.VMEM)
SMEM = pl.BlockSpec(memory_space=pltpu.SMEM)


def taps_of(which):
    return pl.BlockSpec((1, 1, 27, 128, 128), lambda _: (0, which, 0, 0, 0))


def cost(layers):
    flops = layers * CELLS * 27 * 128 * 128 * 2
    return pl.CostEstimate(flops=flops, bytes_accessed=6_000_000, transcendentals=0)


def call(kernel, specs, outs, scratch, layers, out_specs=None, aliases=None):
    return pl.pallas_call(
        kernel,
        grid=(1,),
        in_specs=specs,
        out_specs=out_specs or [VMEM] * len(outs),
        out_shape=[jax.ShapeDtypeStruct(shape, kind) for shape, kind in outs],
        scratch_shapes=[pltpu.VMEM(shape, kind) for shape, kind in scratch],
        input_output_aliases=aliases or {},
        compiler_params=pltpu.CompilerParams(vmem_limit_bytes=VMEM_LIMIT),
        cost_estimate=cost(layers),
    )


def along(block, distance):
    count = lax.axis_size("section")
    return lax.ppermute(block, "section", [((i - distance) % count, i) for i in range(count)])


def halo(low_block, high_block):
    count = lax.axis_size("tile")
    low = lax.ppermute(low_block, "tile", [(i, (i + 1) % count) for i in range(count)])
    high = lax.ppermute(high_block, "tile", [((i + 1) % count, i) for i in range(count)])
    return low, high


def tiles(target):
    route = []
    for i in range(lax.axis_size("tile")):
        deep, near, core = target(i // 4, i // 2 % 2, i % 2)
        route.append((i, (deep % 8) * 4 + near * 2 + core))
    return route


def sent(block, target):
    return lax.ppermute(block, "tile", tiles(target))


def swapped(block):
    return sent(block, lambda z, y, c: (z, y, 1 - c))


def onward(block):
    return sent(block, lambda z, y, c: (z + 1 - 2 * c, y, c))


def tied(*values):
    return lax.optimization_barrier(values)


def updated(momentum, kept, chunks, places, scale):
    count = len(chunks)
    spec = pl.BlockSpec((1, 2, 27, 16, 128), lambda at, places: (0, 0, 0, places[at], 0))
    anywhere = pl.BlockSpec(memory_space=pl.ANY)
    return pl.pallas_call(
        functools.partial(momentum_kernel, scale, count),
        grid_spec=pltpu.PrefetchScalarGridSpec(
            num_scalar_prefetch=1,
            grid=(count,),
            in_specs=[spec] + [pl.BlockSpec((2, 27, 16, 128), lambda at, places: (0, 0, 0, 0))] * count + [anywhere] * len(kept),
            out_specs=spec,
        ),
        out_shape=jax.ShapeDtypeStruct(momentum.shape, f32),
        input_output_aliases={count + 2: 0} if kept else {},
        compiler_params=pltpu.CompilerParams(vmem_limit_bytes=VMEM_LIMIT),
        cost_estimate=pl.CostEstimate(flops=1_000_000, bytes_accessed=1_100_000 * count, transcendentals=0),
    )(places, momentum, *chunks, *kept)


def shards(carried_act, stored_out, cotangent, weights, momentum):
    half = 128
    field = (6, 16, 16, half)
    count = lax.axis_size("tile")
    total = stored_out.shape[1] * count * stored_out.shape[2] * stored_out.shape[3]
    scale = grad_weight / float(total) ** 0.5
    place = lax.axis_index("tile").reshape(1)
    core, deep = place[0] % 2, place[0] // 4
    wide10, wide8 = ((10 * STEP, 384), bf16), ((8 * STEP, 384), bf16)
    taps = ((27 * half, half), bf16)
    flat = ((384, 8 * CELLS), bf16)
    padded, all_d = ((6 * STEP, half), bf16), ((6 * CELLS, 384), bf16)
    eighths, parts = ((4, 2, 27, 16, half), bf16), ((27, half, half), bf16)
    ten, eight = ((10, CELLS, half), bf16), ((8, CELLS, half), bf16)
    whole = ((1, 6, 16, 16, 2 * half), bf16)
    anywhere = pl.BlockSpec(memory_space=pl.ANY)

    z = stored_out[0]
    ends = ((2, 16, 16, 2 * half), bf16)
    top, bottom, c_one, c_two = call(cut_kernel, [VMEM, VMEM], [ends, ends, (field, bf16), (field, bf16)], [], 1)(
        z, cotangent[0]
    )
    z_low, z_high = halo(top, bottom)
    (g_turned,) = call(turned_kernel, [taps_of(1)], [taps], [], 1)(weights)
    c_two, g_turned = tied(c_two, g_turned)
    c_two = along(c_two, -1)
    z_low, z_high, g_turned = tied(z_low, z_high, g_turned)
    g_scale, r = call(
        stored_kernel,
        [SMEM, VMEM, VMEM, VMEM, taps_of(1)],
        [((8, CELLS, half), f32), eight],
        [wide10, taps, ten, eight],
        8,
    )(place, z, z_low, z_high, weights)
    late, r = tied(c_one, r)
    c_one = along(late, -1)
    pg = (c_two.astype(f32) * g_scale[1:7].reshape(field)).astype(bf16)
    pg, r = tied(pg, r)
    pg_low, pg_high = halo(pg[5:], pg[:1])
    f_scale, z_flat, r_flat = call(
        inner_kernel,
        [SMEM, VMEM, VMEM, VMEM, VMEM, taps_of(0)],
        [((6, CELLS, half), f32), flat, flat],
        [wide8, taps, eight],
        6,
    )(place, z, z_low, z_high, r, weights)

    def side(which):
        return pl.BlockSpec((1, 6, 16, 16, half), lambda _: (0, 0, 0, 0, which))

    def part(which):
        return pl.BlockSpec((4, 1, 27, 16, half), lambda _: (0, which, 0, 0, 0))

    mine, other = call(
        grad_g_kernel, [SMEM, VMEM, VMEM], [eighths] * 2, [padded, all_d, parts], 6, [part(1), part(1)]
    )(place, z_flat, pg)
    act, pg_low, pg_high = tied(carried_act[0], pg_low, pg_high)
    a = along(act, 1)
    d_one, pf, mine, other = call(
        first_kernel,
        [SMEM] + [VMEM] * 7 + [anywhere] * 2,
        [whole, (field, bf16), eighths, eighths],
        [wide8, padded, all_d, parts, eight],
        12,
        [side(0), VMEM, part(0), part(0)],
        {8: 2, 9: 3},
    )(place, pg, pg_low, pg_high, c_one, f_scale, g_turned, r_flat, mine, other)

    from_core = swapped(other)
    from_core, weights_later = tied(from_core, weights)
    pf_low, pf_high = halo(pf[5:], pf[:1])

    def own(m):
        return mine[m].astype(f32) + from_core[m].astype(f32)

    sign = jnp.where(core == 0, 7, 1)
    steps = jnp.stack([0 * sign, sign, -sign, 2 * sign, -2 * sign, 3 * sign, -3 * sign, 4 * sign])
    places = (deep + steps + 32) % 8
    got = onward(own(0).astype(bf16))
    owned = [own(m) for m in (1, 2, 3)]
    (f_turned,) = call(turned_kernel, [taps_of(0)], [taps], [], 1)(weights_later)
    got, places, pf_low, pf_high, *owned = tied(got, places, pf_low, pf_high, *owned)
    got = onward((owned[0] + got.astype(f32)).astype(bf16))
    got, f_turned = tied(got, f_turned)
    got = onward((owned[1] + got.astype(f32)).astype(bf16))
    got, a = tied(got, a)
    a_low, a_high = halo(a[4:], a[:2])
    held = (owned[2] + got.astype(f32)).astype(bf16)
    straight = sent(held, lambda z, y, c: (z + 1 - c, y, c))
    across = sent(held, lambda z, y, c: (z + 1 - c, 1 - y, c))
    held = (straight.astype(f32) + across.astype(f32)).astype(bf16)
    held = (held.astype(f32) + swapped(held).astype(f32)).astype(bf16)
    first = onward(held)
    (out_grad,) = call(
        second_kernel, [SMEM] + [VMEM] * 5 + [anywhere], [whole], [wide8, eight], 6, [side(1)], {6: 0}
    )(place, pf, pf_low, pf_high, c_two, f_turned, d_one)
    first, a_low, a_high, out_grad = tied(first, a_low, a_high, out_grad)
    second = onward(first)
    first_other = swapped(first)
    (b_one,) = call(
        b_one_kernel, [SMEM, VMEM, VMEM, VMEM, taps_of(0)], [eight], [wide10, taps, eight, ten], 8
    )(place, a, a_low, a_high, weights)
    second, first_other, b_one = tied(second, first_other, b_one)
    third = onward(second)
    second_other = swapped(second)
    (out_fwd,) = call(b_two_kernel, [VMEM, VMEM, taps_of(1)], [whole], [wide8, taps], 6)(a, b_one, weights)
    third, second_other, out_fwd = tied(third, second_other, out_fwd)
    fourth = onward(third)
    third_other = swapped(third)
    new = updated(momentum, [], [held, first, first_other, second, second_other], places[:5], scale)
    fourth, third_other, new = tied(fourth, third_other, new)
    new = updated(momentum, [new], [third, third_other, fourth], places[5:], scale)
    return (out_fwd, out_grad, new)


def solution(mesh):
    placed = (
        P("section", "tile", None, None, None),
        P("section", "tile", None, None, None),
        P("section", "tile", None, None, None),
        P("section", None, None, None, None),
        P("section", None, None, None, None),
    )
    return jax.shard_map(
        shards,
        mesh=mesh,
        in_specs=placed,
        out_specs=(
            P("section", "tile", None, None, None),
            P("section", "tile", None, None, None),
            P("section", None, None, None, None),
        ),
        check_vma=False,
    )
```
